256 devices in a mesh: rows: 16 (over z, core), delay: 16 (over y, x).
Axes of the slice: x: 4, y: 4, z: 8, core: 2. Of those that a mesh axis runs over, the one named last changes fastest.
Arguments:
- retarded_tiles: bfloat16 [16, 1024, 4, 128, 128], P('delay', 'rows'), may hold values from -0.0625 to 0.0625
- wanted_blocks: int32 [16, 16, 16, 8], P('delay', 'rows'), may hold values from 0 to 63, as said below
- tile_slots: int32 [16, 1024, 4], P('delay', 'rows'), may hold values from 0 to 127, as said below
- diag_inverse: bfloat16 [1024, 128, 128], P('rows')
- excitation: float32 [4, 1024, 4, 128], P(None, 'rows'), may hold values from -6 to 6
- history_init: bfloat16 [16, 1024, 4, 128], P('delay', 'rows'), may hold values from -6 to 6
Outputs:
- currents: float32 [4, 1024, 4, 128], P(None, 'rows')
The draws below stay inside these ranges and needn't reach their ends.
Inputs may be any that keep to these rules, and one draw needn't show every extreme that they name: `wanted_blocks`: for each bin, reader and owner, 8 distinct local block numbers of the owner. `tile_slots`: in each bin, every one of a reader's 16 * 8 taken blocks is the column block of at least one tile of the reader's row blocks.
All inputs are finite; a program needn't handle non-finite values.
Results may differ from the reference program's by a relative error of at most 0.0035.
Values may be sent and summed in bfloat16 or wider, within the bound.
No kernel may reach another device: no remote copies, remote signals or barrier semaphores. Data moves between devices by JAX's collectives and lax.ppermute only.
A program may use at most 64 MiB of HBM per device.

```python
import math
import jax
import jax.numpy as jnp
from jax import lax

B = 128
NB_DEV = 64
L = 4
EXC = 4
STEPS = 4
BINS = 16
N_BLK = 1024
CAP = 8
N_ROWS = 16


def draw_wanted_blocks(key, part):
    scores = jax.random.randint(key, (BINS, N_ROWS, N_ROWS, NB_DEV), 0, 4096) * NB_DEV + jnp.arange(NB_DEV, dtype=jnp.int32)
    ranking = jnp.argsort(scores, axis=-1)
    return ranking[..., :CAP].astype(jnp.int32)


def draw_tile_slots(key, part):
    key_order = jax.random.fold_in(key, 11)
    key_fill = jax.random.fold_in(key, 12)
    spot_count = NB_DEV * L
    received = N_ROWS * CAP
    scores = jax.random.randint(key_order, (BINS, N_ROWS, spot_count), 0, 4096) * spot_count + jnp.arange(spot_count, dtype=jnp.int32)
    ranking = jnp.argsort(scores, axis=-1).astype(jnp.int32)
    filler = jax.random.randint(key_fill, (BINS, N_ROWS, spot_count), 0, received)
    values = jnp.where(ranking < received, ranking, filler)
    return values.reshape(BINS, N_BLK, L).astype(jnp.int32)


def draw_diag_inverse(key, part):
    noise = jax.random.normal(key, (N_BLK, B, B), jnp.float32)
    identity = jnp.eye(B, dtype=jnp.float32)
    return (identity + 0.3 * noise / math.sqrt(B)).astype(jnp.bfloat16)


def block_levels(stream_key, shape, cuts, low, largest):
    def one(axis_at, parts):
        steps = jax.random.uniform(jax.random.fold_in(jax.random.fold_in(stream_key, 6), axis_at), (parts,), jnp.float32, low / len(cuts), largest / len(cuts))
        return jnp.repeat(jnp.exp(steps), shape[axis_at] // parts).reshape((-1,) + (1,) * (len(shape) - axis_at - 1))

    loudness = one(*cuts[0])
    for cut in cuts[1:]:
        loudness = loudness * one(*cut)
    return loudness


def bell_draw(stream_key, dims, scale, most, split=(), kind=jnp.bfloat16):
    result = jax.random.normal(stream_key, dims, jnp.float32) * scale
    if len(split) > 0:
        result = block_levels(stream_key, dims, split, -0.22, 0.18) * result
    return jnp.clip(result, min=-most, max=most).astype(kind)


def setup_inputs(seed: int = 0) -> dict:
    seeds = jax.random.split(jax.random.key(seed), 7)
    retarded_tiles = bell_draw(seeds[0], (BINS, N_BLK, L, B, B), (B * L * BINS) ** -0.5, 0.0625, ((0, 16), (1, 16)))
    wanted_blocks = draw_wanted_blocks(jax.random.fold_in(seeds[6], 71), 0)
    tile_slots = draw_tile_slots(jax.random.fold_in(seeds[6], 71), 0)
    diag_inverse = draw_diag_inverse(jax.random.fold_in(seeds[6], 71), 0)
    excitation = bell_draw(seeds[4], (STEPS, N_BLK, EXC, B), 1.0, 6.0, ((1, 16),), jnp.float32)
    history_init = bell_draw(seeds[5], (BINS, N_BLK, EXC, B), 1.0, 6.0, ((0, 16), (1, 16)))
    return {"retarded_tiles": retarded_tiles, "wanted_blocks": wanted_blocks, "tile_slots": tile_slots, "diag_inverse": diag_inverse, "excitation": excitation, "history_init": history_init}


def bin_term(hist_bin, tile_bin, column_bin):
    blocks = hist_bin[column_bin.astype(jnp.int32)].astype(jnp.float32)
    return jnp.einsum('nleb,nlbc->nec', blocks, tile_bin.astype(jnp.float32))


def reference(retarded_tiles, wanted_blocks, tile_slots, diag_inverse, excitation, history_init):
    owners = tile_slots // CAP
    within = tile_slots % CAP
    readers = (jnp.arange(N_BLK, dtype=jnp.int32) // NB_DEV)[None, :, None]
    bin_index = jnp.arange(BINS, dtype=jnp.int32)[:, None, None]
    columns = (owners * NB_DEV + wanted_blocks[bin_index, readers, owners, within]).astype(jnp.int32)
    history = history_init
    results = []
    for moment in range(STEPS):
        def add_bin(total, item):
            hist_bin, tile_bin, column_bin = item
            return total + bin_term(hist_bin, tile_bin, column_bin), None

        retarded, _ = lax.scan(add_bin, jnp.zeros((N_BLK, EXC, B), jnp.float32), (history, retarded_tiles, columns))
        driven = (excitation[moment] - retarded).astype(jnp.bfloat16)
        solved = jnp.einsum('neb,nbc->nec', driven.astype(jnp.float32), diag_inverse.astype(jnp.float32))
        results.append(solved)
        history = jnp.concatenate([solved.astype(jnp.bfloat16)[None], history[:-1]], axis=0)
    return jnp.stack(results)
```

```python
import jax
import jax.numpy as jnp
from jax import lax
from jax.experimental import pallas as pl
from jax.experimental.pallas import tpu as pltpu
from jax.sharding import PartitionSpec as P

STEPS = 4
LANES = 16
ROWS = 16
CAP = 8
NB = 64
EXC = 4
B = 128
L = 4
TAKEN = ROWS * CAP
FLAT = NB * EXC
SPARE = (4, 5, 6)
GROUP = 8

bf16 = jnp.bfloat16
f32 = jnp.float32
VMEM = pl.BlockSpec(memory_space=pltpu.VMEM)
SMEM = pl.BlockSpec(memory_space=pltpu.SMEM)
LIMIT = 24 * 1024 * 1024


def call(kernel, out_shape, scratch, operands, in_smem, name):
    specs = [SMEM if i in in_smem else VMEM for i in range(len(operands))]
    many = isinstance(out_shape, (tuple, list))
    return pl.pallas_call(
        kernel,
        out_shape=out_shape,
        in_specs=specs,
        out_specs=[VMEM] * len(out_shape) if many else VMEM,
        scratch_shapes=scratch,
        compiler_params=pltpu.CompilerParams(vmem_limit_bytes=LIMIT),
        name=name,
    )(*operands)


def pick_initial(asked, h0, h1, h2, h3, out, wide, packed):
    for t, h in enumerate((h0, h1, h2, h3)):
        wide[:, EXC * t : EXC * (t + 1), :] = h[...].astype(f32)
    packed[...] = wide[...].astype(bf16)

    @pl.loop(0, ROWS)
    def _(r):
        for p in range(CAP):
            out[r * CAP + p] = packed[asked[r, p]]


def initial_terms(slots, tiles, arrived, out, total):
    @pl.loop(0, NB // GROUP)
    def _(g):
        for j in range(GROUP):
            i = g * GROUP + j
            row = jnp.concatenate([arrived[slots[s, i]] for s in range(L)], axis=1)
            tile = tiles[i].reshape(L * B, B)
            term = jnp.dot(row, tile, preferred_element_type=f32)
            at = pl.multiple_of(g * GROUP * EXC, GROUP * EXC)
            for t in range(STEPS):
                total[t, pl.ds(at + EXC * j, EXC), :] = term[EXC * t : EXC * (t + 1)]

    for t in range(STEPS):
        value = total[t].astype(bf16)
        if t == 0:
            for lane in range(LANES):
                if lane not in SPARE:
                    out[lane] = value
        else:
            out[SPARE[t - 1]] = value


def solve_and_pick(asked, driven, diag, solved, send):
    for i in range(NB):
        row = driven[EXC * i : EXC * (i + 1), :].astype(bf16)
        solved[i] = jnp.dot(row, diag[i], preferred_element_type=f32)

    @pl.loop(0, ROWS)
    def _(r):
        for p in range(CAP):
            send[r * CAP + p] = solved[asked[r, p]].astype(bf16)


def first_step(lane, asked, terms, excite, diag, item, send, driven, solved):
    total = terms[0].astype(f32)
    for k in range(1, LANES):
        total = total + terms[k].astype(f32)
    value = excite[...] - total
    driven[...] = value
    me = lane[0]
    spare = (me >= SPARE[0]) & (me <= SPARE[-1])
    item[...] = jnp.where(spare, total, value).astype(bf16)
    solve_and_pick(asked, driven, diag, solved, send)


def tile_terms(slots, tiles, arrived, total):
    @pl.loop(0, NB // GROUP)
    def _(g):
        for j in range(GROUP):
            i = g * GROUP + j
            row = jnp.concatenate([arrived[slots[s, i]] for s in range(L)], axis=1)
            tile = tiles[i].reshape(L * B, B)
            at = pl.multiple_of(g * GROUP * EXC, GROUP * EXC)
            total[pl.ds(at + EXC * j, EXC), :] = jnp.dot(row, tile, preferred_element_type=f32)


def second_step(lane, asked, slots, tiles, arrived, extra, excite, diag, item, send, total, driven, solved):
    tile_terms(slots, tiles, arrived, total)
    value = total[...] + extra[...].astype(f32)
    rest = excite[...] - value
    driven[...] = rest
    item[...] = jnp.where(lane[0] == 0, rest, value).astype(bf16)
    solve_and_pick(asked, driven, diag, solved, send)


def third_step(lane, asked, slots, tiles, arrived, extra, held, excite, diag, item, send, total, driven, solved):
    tile_terms(slots, tiles, arrived, total)
    me = lane[0]
    came = extra[...].astype(f32)
    rest = jnp.where(me == 0, excite[...] - (total[...] + came), came)
    driven[...] = rest
    item[...] = jnp.where(me == 2, held[...].astype(f32), rest).astype(bf16)
    solve_and_pick(asked, driven, diag, solved, send)


def fourth_step(lane, slots, tiles, arrived, extra, out, total):
    tile_terms(slots, tiles, arrived, total)
    me = lane[0]
    came = extra[...].astype(f32)
    value = jnp.where(me == 0, total[...], jnp.where(me == 1, total[...] + came, came)).astype(bf16)
    for y in range(4):
        out[y] = value


def last_solve(item0, items, excite, diag, out, driven):
    driven[0] = item0[...].astype(f32)
    driven[1] = items[2].astype(f32)
    driven[2] = items[3].astype(f32)
    driven[3] = excite[...] - (items[0].astype(f32) + items[1].astype(f32))
    for i in range(NB):
        rows = [driven[t, EXC * i : EXC * (i + 1), :] for t in range(STEPS)]
        both = jnp.concatenate(rows, axis=0).astype(bf16)
        value = jnp.dot(both, diag[i], preferred_element_type=f32)
        for t in range(STEPS):
            out[t, i] = value[EXC * t : EXC * (t + 1)]


def shifted(array, axis, by):
    peers = lax.axis_size(axis)
    return lax.ppermute(array, axis, [(i, i + by) for i in range(peers - by)])


def exchange(array, axis, groups=None):
    return lax.all_to_all(array, axis, split_axis=0, concat_axis=0, tiled=True, axis_index_groups=groups)


def body(retarded_tiles, wanted_blocks, tile_slots, diag_inverse, excitation, history_init):
    sds = jax.ShapeDtypeStruct
    tiles = retarded_tiles[0]
    slots = tile_slots[0].T
    lane = lax.axis_index("delay").astype(jnp.int32).reshape(1)
    excite = excitation.reshape(STEPS, FLAT, B)

    asked = exchange(wanted_blocks[0, 0], "rows")
    h0 = history_init[0]
    later = [shifted(h0, "delay", t) for t in range(1, STEPS)]

    picked = call(
        pick_initial,
        sds((TAKEN, EXC * STEPS, B), bf16),
        [pltpu.VMEM((NB, EXC * STEPS, B), f32), pltpu.VMEM((NB, EXC * STEPS, B), bf16)],
        (asked, h0, *later),
        (0,),
        "pick_initial",
    )
    arrived = exchange(picked.reshape(ROWS, CAP, EXC * STEPS, B), "rows").reshape(TAKEN, EXC * STEPS, B)
    terms = call(
        initial_terms,
        sds((LANES, FLAT, B), bf16),
        [pltpu.VMEM((STEPS, FLAT, B), f32)],
        (slots, tiles, arrived),
        (0,),
        "initial_terms",
    )
    terms = exchange(terms, "delay")

    flat = pltpu.VMEM((FLAT, B), f32)
    block = pltpu.VMEM((NB, EXC, B), f32)
    outs = (sds((FLAT, B), bf16), sds((TAKEN, EXC, B), bf16))

    item, send = call(
        first_step, outs, [flat, block], (lane, asked, terms, excite[0], diag_inverse), (0, 1), "first_step"
    )
    came = lax.ppermute(item, "delay", [(4, 0), (5, 1), (6, 2), (0, 4), (1, 5), (2, 6)])
    arrived = exchange(send.reshape(ROWS, CAP, EXC, B), "rows").reshape(TAKEN, EXC, B)
    me = lane[0]
    item0 = jnp.where((me >= SPARE[0]) & (me <= SPARE[-1]), came, item)

    item1, send = call(
        second_step,
        outs,
        [flat, flat, block],
        (lane, asked, slots, tiles, arrived, came, excite[1], diag_inverse),
        (0, 1, 2),
        "second_step",
    )
    came = lax.ppermute(item1, "delay", [(0, 1), (1, 0)])
    arrived = exchange(send.reshape(ROWS, CAP, EXC, B), "rows").reshape(TAKEN, EXC, B)

    item2, send = call(
        third_step,
        outs,
        [flat, flat, block],
        (lane, asked, slots, tiles, arrived, came, item1, excite[2], diag_inverse),
        (0, 1, 2),
        "third_step",
    )
    came = lax.ppermute(item2, "delay", [(0, 3), (1, 2), (2, 1)])
    arrived = exchange(send.reshape(ROWS, CAP, EXC, B), "rows").reshape(TAKEN, EXC, B)

    item3 = call(
        fourth_step,
        sds((4, FLAT, B), bf16),
        [flat],
        (lane, slots, tiles, arrived, came),
        (0, 1),
        "fourth_step",
    )
    along_y = [[4 * y + x for y in range(4)] for x in range(4)]
    along_x = [[4 * y + x for x in range(4)] for y in range(4)]
    column = exchange(item3, "delay", along_y)[0]
    items = exchange(jnp.broadcast_to(column, (4, FLAT, B)), "delay", along_x)
    return call(
        last_solve,
        sds((STEPS, NB, EXC, B), f32),
        [pltpu.VMEM((STEPS, FLAT, B), f32)],
        (item0, items, excite[3], diag_inverse),
        (),
        "last_solve",
    )


def solution(mesh):
    return jax.shard_map(
        body,
        mesh=mesh,
        in_specs=(
            P("delay", "rows", None, None, None),
            P("delay", "rows", None, None),
            P("delay", "rows", None),
            P("rows", None, None),
            P(None, "rows", None, None),
            P("delay", "rows", None, None),
        ),
        out_specs=P(None, "rows", None, None),
        check_vma=False,
    )
```

```python
import jax
import jax.numpy as jnp
from jax import lax
from jax.experimental import pallas as pl
from jax.experimental.pallas import tpu as pltpu
from jax.sharding import PartitionSpec as P


STEPS = 4
LANES = 16
ROWS = 16
CAP = 8
NB = 64
EXC = 4
B = 128
L = 4
TAKEN = ROWS * CAP
FLAT = NB * EXC
SPARE = (4, 5, 6)
GROUP = 8

bf16 = jnp.bfloat16
f32 = jnp.float32
VMEM = pl.BlockSpec(memory_space=pltpu.VMEM)
SMEM = pl.BlockSpec(memory_space=pltpu.SMEM)
LIMIT = 24 * 1024 * 1024


def call(kernel, out_shape, scratch, operands, in_smem):
    specs = [SMEM if i in in_smem else VMEM for i in range(len(operands))]
    many = isinstance(out_shape, (tuple, list))
    return pl.pallas_call(
        kernel,
        out_shape=out_shape,
        in_specs=specs,
        out_specs=[VMEM] * len(out_shape) if many else VMEM,
        scratch_shapes=scratch,
        compiler_params=pltpu.CompilerParams(vmem_limit_bytes=LIMIT),
    )(*operands)


def pick_initial(lane, asked, h0, h1, h2, h3, out, wide, packed):
    for t, h in enumerate((h0, h1, h2, h3)):
        wide[:, EXC * t : EXC * (t + 1), :] = h[...].astype(f32)
    packed[...] = wide[...].astype(bf16)

    @pl.loop(0, ROWS)
    def _(r):
        for p in range(CAP):
            out[r * CAP + p] = packed[asked[r, p]]


def initial_terms(slots, tiles, arrived, out, total):
    @pl.loop(0, NB // GROUP)
    def _(g):
        for j in range(GROUP):
            i = g * GROUP + j
            row = jnp.concatenate([arrived[slots[s, i]] for s in range(L)], axis=1)
            tile = tiles[i].reshape(L * B, B)
            term = jnp.dot(row, tile, preferred_element_type=f32)
            at = pl.multiple_of(g * GROUP * EXC, GROUP * EXC)
            for t in range(STEPS):
                total[t, pl.ds(at + EXC * j, EXC), :] = term[EXC * t : EXC * (t + 1)]

    for t in range(STEPS):
        value = total[t].astype(bf16)
        if t == 0:
            for lane in range(LANES):
                if lane not in SPARE:
                    out[lane] = value
        else:
            out[SPARE[t - 1]] = value


def solve_and_pick(asked, driven, diag, solved, send):
    for i in range(NB):
        row = driven[EXC * i : EXC * (i + 1), :].astype(bf16)
        solved[i] = jnp.dot(row, diag[i], preferred_element_type=f32)

    @pl.loop(0, ROWS)
    def _(r):
        for p in range(CAP):
            send[r * CAP + p] = solved[asked[r, p]].astype(bf16)


def first_step(lane, asked, terms, excite, diag, item, send, driven, solved):
    total = terms[0].astype(f32)
    for k in range(1, LANES):
        total = total + terms[k].astype(f32)
    value = excite[0] - total
    driven[...] = value
    me = lane[0]
    spare = (me >= SPARE[0]) & (me <= SPARE[-1])
    item[...] = jnp.where(spare, total, value).astype(bf16)
    solve_and_pick(asked, driven, diag, solved, send)


def tile_terms(slots, tiles, arrived, total):
    @pl.loop(0, NB // GROUP)
    def _(g):
        for j in range(GROUP):
            i = g * GROUP + j
            row = jnp.concatenate([arrived[slots[s, i]] for s in range(L)], axis=1)
            tile = tiles[i].reshape(L * B, B)
            at = pl.multiple_of(g * GROUP * EXC, GROUP * EXC)
            total[pl.ds(at + EXC * j, EXC), :] = jnp.dot(row, tile, preferred_element_type=f32)


def second_step(lane, asked, total, extra, excite, diag, item, send, driven, solved):
    value = total[...] + extra[...].astype(f32)
    rest = excite[1] - value
    driven[...] = rest
    item[...] = jnp.where(lane[0] == 0, rest, value).astype(bf16)
    solve_and_pick(asked, driven, diag, solved, send)


def third_step(lane, asked, total, extra, held, excite, diag, item, send, driven, solved):
    me = lane[0]
    came = extra[...].astype(f32)
    rest = jnp.where(me == 0, excite[2] - (total[...] + came), came)
    driven[...] = rest
    item[...] = jnp.where(me == 2, held[...].astype(f32), rest).astype(bf16)
    solve_and_pick(asked, driven, diag, solved, send)


def fourth_step(lane, total, extra, out):
    me = lane[0]
    came = extra[...].astype(f32)
    value = jnp.where(me == 0, total[...], jnp.where(me == 1, total[...] + came, came)).astype(bf16)
    for y in range(4):
        out[y] = value


def repeat(column, out):
    for x in range(4):
        out[x] = column[0]


def last_solve(lane, item0, came, items, excite, diag, out, driven):
    me = lane[0]
    spare = (me >= SPARE[0]) & (me <= SPARE[-1])
    driven[0] = jnp.where(spare, came[...].astype(f32), item0[...].astype(f32))
    driven[1] = items[2].astype(f32)
    driven[2] = items[3].astype(f32)
    driven[3] = excite[3] - (items[0].astype(f32) + items[1].astype(f32))
    for i in range(NB):
        rows = [driven[t, EXC * i : EXC * (i + 1), :] for t in range(STEPS)]
        both = jnp.concatenate(rows, axis=0).astype(bf16)
        value = jnp.dot(both, diag[i], preferred_element_type=f32)
        for t in range(STEPS):
            out[t, i] = value[EXC * t : EXC * (t + 1)]


def shifted(array, axis, by):
    peers = lax.axis_size(axis)
    return lax.ppermute(array, axis, [(i, i + by) for i in range(peers - by)])


def exchange(array, axis, groups=None):
    return lax.all_to_all(array, axis, split_axis=0, concat_axis=0, tiled=True, axis_index_groups=groups)


def body(retarded_tiles, wanted_blocks, tile_slots, diag_inverse, excitation, history_init):
    sds = jax.ShapeDtypeStruct
    tiles = retarded_tiles[0]
    slots = tile_slots[0].T
    lane = lax.axis_index("delay").astype(jnp.int32).reshape(1)
    excite = excitation.reshape(STEPS, FLAT, B)

    asked = exchange(wanted_blocks[0, 0], "rows")
    h0 = history_init[0]
    later = []
    for t in range(1, STEPS):
        later.append(shifted(h0, "delay", t))

    picked = call(
        pick_initial,
        sds((TAKEN, EXC * STEPS, B), bf16),
        [pltpu.VMEM((NB, EXC * STEPS, B), f32), pltpu.VMEM((NB, EXC * STEPS, B), bf16)],
        (lane, asked, h0, *later),
        (0, 1),
    )
    arrived = exchange(picked.reshape(ROWS, CAP, EXC * STEPS, B), "rows").reshape(TAKEN, EXC * STEPS, B)
    terms = call(
        initial_terms,
        sds((LANES, FLAT, B), bf16),
        [pltpu.VMEM((STEPS, FLAT, B), f32)],
        (slots, tiles, arrived),
        (0,),
    )
    terms = exchange(terms, "delay")

    flat = pltpu.VMEM((FLAT, B), f32)
    block = pltpu.VMEM((NB, EXC, B), f32)
    outs = (sds((FLAT, B), bf16), sds((TAKEN, EXC, B), bf16))

    item0, send = call(
        first_step, outs, [flat, block], (lane, asked, terms, excite, diag_inverse), (0, 1)
    )
    came0 = lax.ppermute(item0, "delay", [(4, 0), (5, 1), (6, 2), (0, 4), (1, 5), (2, 6)])
    arrived = exchange(send.reshape(ROWS, CAP, EXC, B), "rows").reshape(TAKEN, EXC, B)
    total = call(tile_terms, sds((FLAT, B), f32), [], (slots, tiles, arrived), (0,))

    item1, send = call(
        second_step, outs, [flat, block], (lane, asked, total, came0, excite, diag_inverse), (0, 1)
    )
    came = lax.ppermute(item1, "delay", [(0, 1), (1, 0)])
    arrived = exchange(send.reshape(ROWS, CAP, EXC, B), "rows").reshape(TAKEN, EXC, B)
    total = call(tile_terms, sds((FLAT, B), f32), [], (slots, tiles, arrived), (0,))

    item2, send = call(
        third_step,
        outs,
        [flat, block],
        (lane, asked, total, came, item1, excite, diag_inverse),
        (0, 1),
    )
    came = lax.ppermute(item2, "delay", [(0, 3), (1, 2), (2, 1)])
    arrived = exchange(send.reshape(ROWS, CAP, EXC, B), "rows").reshape(TAKEN, EXC, B)
    total = call(tile_terms, sds((FLAT, B), f32), [], (slots, tiles, arrived), (0,))

    item3 = call(fourth_step, sds((4, FLAT, B), bf16), [], (lane, total, came), (0,))
    along_y = [[4 * y + x for y in range(4)] for x in range(4)]
    along_x = [[4 * y + x for x in range(4)] for y in range(4)]
    column = exchange(item3, "delay", along_y)
    column = call(repeat, sds((4, FLAT, B), bf16), [], (column,), ())
    items = exchange(column, "delay", along_x)
    return call(
        last_solve,
        sds((STEPS, NB, EXC, B), f32),
        [pltpu.VMEM((STEPS, FLAT, B), f32)],
        (lane, item0, came0, items, excite, diag_inverse),
        (0,),
    )


def solution(mesh):
    return jax.shard_map(
        body,
        mesh=mesh,
        in_specs=(
            P("delay", "rows", None, None, None),
            P("delay", "rows", None, None),
            P("delay", "rows", None),
            P("rows", None, None),
            P(None, "rows", None, None),
            P("delay", "rows", None, None),
        ),
        out_specs=P(None, "rows", None, None),
        check_vma=False,
    )
```

```python
import jax
import jax.numpy as jnp
from jax import lax
from jax.experimental import pallas as pl
from jax.experimental.pallas import tpu as pltpu
from jax.sharding import PartitionSpec as P


STEPS = 4
LANES = 16
ROWS = 16
CAP = 8
NB = 64
EXC = 4
B = 128
L = 4
TAKEN = ROWS * CAP
FLAT = NB * EXC
KNOWN = 3
SHARE = FLAT // LANES
PART = FLAT // 4
GROUP = 8

bf16 = jnp.bfloat16
f32 = jnp.float32
VMEM = pl.BlockSpec(memory_space=pltpu.VMEM)
SMEM = pl.BlockSpec(memory_space=pltpu.SMEM)
HBM = pl.BlockSpec(memory_space=pltpu.HBM)
LIMIT = 24 * 1024 * 1024


def call(kernel, out_shape, scratch, operands, in_smem, in_place=()):
    specs = [SMEM if i in in_smem else HBM if i in in_place else VMEM for i in range(len(operands))]
    many = isinstance(out_shape, (tuple, list))
    operands = [pltpu.with_memory_space_constraint(x, pltpu.HBM) if i in in_place else x for i, x in enumerate(operands)]
    return pl.pallas_call(
        kernel,
        out_shape=out_shape,
        in_specs=specs,
        out_specs=[VMEM] * len(out_shape) if many else VMEM,
        scratch_shapes=scratch,
        compiler_params=pltpu.CompilerParams(vmem_limit_bytes=LIMIT),
    )(*operands)


def pick_initial(lane, asked, stored, h1, h2, out, h0, sem):
    copy = pltpu.make_async_copy(stored, h0, sem)
    copy.start()

    @pl.loop(0, ROWS)
    def _(r):
        for t, h in enumerate((h1, h2)):
            for p in range(CAP):
                out[r, (t + 1) * CAP + p] = h[asked[r, p]]

    copy.wait()

    @pl.loop(0, ROWS)
    def _(r):
        for p in range(CAP):
            out[r, p] = h0[asked[r, p]]


def initial_terms(listed, stored, arrived, out, tiles, slots, wide, packed, total, sem, sems):
    lists = pltpu.make_async_copy(listed, slots, sem)
    lists.start()
    copies = []
    for g in range(NB // GROUP):
        part = pl.ds(g * GROUP, GROUP)
        copies.append(pltpu.make_async_copy(stored.at[part], tiles.at[part], sems.at[g]))
        copies[-1].start()
    for o in range(ROWS):
        for t in range(KNOWN):
            here = arrived[o, CAP * t : CAP * (t + 1)]
            wide[CAP * o : CAP * (o + 1), EXC * t : EXC * (t + 1), :] = here.astype(f32)
    packed[...] = wide[...].astype(bf16)
    lists.wait()

    for g in range(NB // GROUP):
        copies[g].wait()
        for j in range(GROUP):
            i = g * GROUP + j
            row = jnp.concatenate([packed[slots[s, i]] for s in range(L)], axis=1)
            tile = tiles[i].reshape(L * B, B)
            term = jnp.dot(row, tile, preferred_element_type=f32)
            for t in range(KNOWN):
                total[t, EXC * i : EXC * (i + 1), :] = term[EXC * t : EXC * (t + 1)]

    for y in range(4):
        for x in range(4):
            out[4 * y + x] = total[y % KNOWN, PART * x : PART * (x + 1), :].astype(bf16)


def add_terms(terms, out):
    total = terms[0].astype(f32)
    for k in range(1, LANES):
        total = total + terms[k].astype(f32)
    for x in range(4):
        out[x] = total


def solve(driven, diag, solved):
    for i in range(NB):
        row = driven[EXC * i : EXC * (i + 1), :].astype(bf16)
        solved[i] = jnp.dot(row, diag[i], preferred_element_type=f32)


def pick(asked, solved, send):
    @pl.loop(0, ROWS)
    def _(r):
        for p in range(CAP):
            send[r, p] = solved[asked[r, p]].astype(bf16)


def first_step(lane, asked, total, excite, diag, item, send, driven, solved):
    driven[...] = excite[0] - total[...]
    item[...] = driven[...].astype(bf16)
    solve(driven, diag, solved)
    pick(asked, solved, send)


def tile_terms(slots, tiles, arrived, total):
    @pl.loop(0, NB // GROUP)
    def _(g):
        for j in range(GROUP):
            i = g * GROUP + j
            row = jnp.concatenate([arrived[slots[s, i]] for s in range(L)], axis=1)
            tile = tiles[i].reshape(L * B, B)
            at = pl.multiple_of(g * GROUP * EXC, GROUP * EXC)
            total[pl.ds(at + EXC * j, EXC), :] = jnp.dot(row, tile, preferred_element_type=f32)


def second_step(lane, asked, total, came, h2, excite, diag, item, send, driven, solved):
    me = lane[0]
    value = total[...] + came[...]
    driven[...] = excite[1] - value

    @pl.when(me == 0)
    def _():
        item[...] = driven[...].astype(bf16).astype(f32)
        solve(driven, diag, solved)
        pick(asked, solved, send)

    @pl.when(me == 1)
    def _():
        item[...] = value

    @pl.when(me > 1)
    def _():
        for i in range(NB):
            item[EXC * i : EXC * (i + 1), :] = h2[i].astype(f32)


def third_step(lane, asked, total, came, first, excite, diag, item, send, driven, solved):
    me = lane[0]
    other = jnp.where(me == 2, first[...].astype(f32), came[...])
    driven[...] = jnp.where(me == 0, excite[2] - (total[...] + came[...]), other)
    item[...] = driven[...].astype(bf16)

    @pl.when(me < KNOWN)
    def _():
        solve(driven, diag, solved)

    @pl.when(me >= KNOWN)
    def _():
        for i in range(NB):
            solved[i] = driven[EXC * i : EXC * (i + 1), :]

    pick(asked, solved, send)


def fourth_step(slots, tiles, arrived, item, out, total):
    tile_terms(slots, tiles, arrived, total)
    for k in range(LANES):
        mine = slice(SHARE * k, SHARE * (k + 1))
        out[k, :SHARE] = total[mine, :].astype(bf16)
        out[k, SHARE:] = item[mine, :]


def share_driven(lane, parts, excite, out):
    total = parts[0, :SHARE].astype(f32)
    for k in range(1, LANES):
        total = total + parts[k, :SHARE].astype(f32)
    start = pl.multiple_of(lane[0] * SHARE, SHARE)
    last = (excite[STEPS - 1, pl.ds(start, SHARE), :] - total).astype(bf16)
    for k in range(LANES):
        for t in range(STEPS - 1):
            out[k, SHARE * t : SHARE * (t + 1)] = parts[STEPS - 2 - t, SHARE:]
        out[k, SHARE * (STEPS - 1) :] = last


def last_solve(driven, diag, out):
    each = SHARE // EXC
    for i in range(NB):
        value = jnp.dot(driven[i // each], diag[i], preferred_element_type=f32)
        for t in range(STEPS):
            at = SHARE * t + EXC * (i % each)
            out[t, i] = value[at : at + EXC]


def shifted(array, axis, by):
    peers = lax.axis_size(axis)
    return lax.ppermute(array, axis, [(i, i + by) for i in range(peers - by)])


def exchange(array, axis, groups=None):
    return lax.all_to_all(array, axis, split_axis=0, concat_axis=0, tiled=True, axis_index_groups=groups)


def body(retarded_tiles, wanted_blocks, tile_slots, diag_inverse, excitation, history_init):
    sds = jax.ShapeDtypeStruct
    stored = retarded_tiles[0]
    slots = tile_slots[0].T
    lane = lax.axis_index("delay").astype(jnp.int32).reshape(1)
    excite = excitation.reshape(STEPS, FLAT, B)

    asked = exchange(wanted_blocks[0, 0], "rows")
    h0 = history_init[0]
    later = []
    for t in range(1, KNOWN):
        later.append(shifted(h0, "delay", t))

    picked = call(
        pick_initial,
        sds((ROWS, KNOWN * CAP, EXC, B), bf16),
        [pltpu.VMEM(h0.shape, bf16), pltpu.SemaphoreType.DMA],
        (lane, asked, h0, *later),
        (0, 1),
        (2,),
    )
    arrived = exchange(picked, "rows")
    wide = (TAKEN, EXC * STEPS, B)
    terms, tiles = call(
        initial_terms,
        (sds((LANES, PART, B), bf16), sds(stored.shape, bf16)),
        [
            pltpu.SMEM(slots.shape, jnp.int32),
            pltpu.VMEM(wide, f32),
            pltpu.VMEM(wide, bf16),
            pltpu.VMEM((KNOWN, FLAT, B), f32),
            pltpu.SemaphoreType.DMA,
            pltpu.SemaphoreType.DMA((NB // GROUP,)),
        ],
        (slots, stored, arrived),
        (),
        (0, 1),
    )
    terms = exchange(terms, "delay")
    part = call(add_terms, sds((4, PART, B), f32), [], (terms,), ())
    along_x = [[4 * y + x for x in range(4)] for y in range(4)]
    whole = exchange(part, "delay", along_x).reshape(FLAT, B)

    flat = pltpu.VMEM((FLAT, B), f32)
    block = pltpu.VMEM((NB, EXC, B), f32)
    send_shape = sds((ROWS, CAP, EXC, B), bf16)

    came = lax.ppermute(whole, "delay", [(4, 0), (9, 1)])
    item0, send = call(
        first_step,
        (sds((FLAT, B), bf16), send_shape),
        [flat, block],
        (lane, asked, whole, excite, diag_inverse),
        (0, 1),
    )
    arrived = exchange(send, "rows").reshape(TAKEN, EXC, B)
    total = call(tile_terms, sds((FLAT, B), f32), [], (slots, tiles, arrived), (0,))

    item1, send = call(
        second_step,
        (sds((FLAT, B), f32), send_shape),
        [flat, block],
        (lane, asked, total, came, later[1], excite, diag_inverse),
        (0, 1),
    )
    came = lax.ppermute(item1, "delay", [(0, 1), (1, 0)] + [(k, k + 1) for k in range(2, LANES - 1)])
    arrived = exchange(send, "rows").reshape(TAKEN, EXC, B)
    total = call(tile_terms, sds((FLAT, B), f32), [], (slots, tiles, arrived), (0,))

    item2, send = call(
        third_step,
        (sds((FLAT, B), bf16), send_shape),
        [flat, block],
        (lane, asked, total, came, item0, excite, diag_inverse),
        (0, 1),
    )
    arrived = exchange(send, "rows").reshape(TAKEN, EXC, B)
    parts = call(
        fourth_step, sds((LANES, 2 * SHARE, B), bf16), [flat], (slots, tiles, arrived, item2), (0,)
    )
    parts = exchange(parts, "delay")
    shares = call(
        share_driven, sds((LANES, STEPS * SHARE, B), bf16), [], (lane, parts, excite), (0,)
    )
    driven = exchange(shares, "delay")
    return call(last_solve, sds((STEPS, NB, EXC, B), f32), [], (driven, diag_inverse), ())


def solution(mesh):
    return jax.shard_map(
        body,
        mesh=mesh,
        in_specs=(
            P("delay", "rows", None, None, None),
            P("delay", "rows", None, None),
            P("delay", "rows", None),
            P("rows", None, None),
            P(None, "rows", None, None),
            P("delay", "rows", None, None),
        ),
        out_specs=P(None, "rows", None, None),
        check_vma=False,
    )
```

```python
import jax
import jax.numpy as jnp
from jax import lax
from jax.experimental import pallas as pl
from jax.experimental.pallas import tpu as pltpu
from jax.sharding import PartitionSpec as P


STEPS = 4
LANES = 16
ROWS = 16
CAP = 8
NB = 64
EXC = 4
B = 128
L = 4
TAKEN = ROWS * CAP
FLAT = NB * EXC
KNOWN = 3
SHARE = FLAT // LANES
PART = FLAT // 4
GROUP = 8

bf16 = jnp.bfloat16
f32 = jnp.float32
VMEM = pl.BlockSpec(memory_space=pltpu.VMEM)
SMEM = pl.BlockSpec(memory_space=pltpu.SMEM)
HBM = pl.BlockSpec(memory_space=pltpu.HBM)
LIMIT = 24 * 1024 * 1024


def call(kernel, out_shape, scratch, operands, in_smem, in_place=()):
    specs = [SMEM if i in in_smem else HBM if i in in_place else VMEM for i in range(len(operands))]
    many = isinstance(out_shape, (tuple, list))
    operands = [pltpu.with_memory_space_constraint(x, pltpu.HBM) if i in in_place else x for i, x in enumerate(operands)]
    return pl.pallas_call(
        kernel,
        out_shape=out_shape,
        in_specs=specs,
        out_specs=[VMEM] * len(out_shape) if many else VMEM,
        scratch_shapes=scratch,
        compiler_params=pltpu.CompilerParams(vmem_limit_bytes=LIMIT),
    )(*operands)


def pick_initial(asked, stored, h1, h2, out, h0, sem):
    copy = pltpu.make_async_copy(stored, h0, sem)
    copy.start()

    for r in range(ROWS):
        for p in range(CAP):
            at = asked[r, p]
            out[r, CAP + p] = h1[at]
            out[r, 2 * CAP + p] = h2[at]
    copy.wait()
    for r in range(ROWS):
        for p in range(CAP):
            out[r, p] = h0[asked[r, p]]


def initial_terms(listed, stored, arrived, out, tiles, slots, wide, packed, total, sem, sems):
    lists = pltpu.make_async_copy(listed, slots, sem)
    lists.start()
    copies = []
    for g in range(NB // GROUP):
        part = pl.ds(g * GROUP, GROUP)
        copies.append(pltpu.make_async_copy(stored.at[part], tiles.at[part], sems.at[g]))
        copies[-1].start()
    for o in range(ROWS):
        for t in range(KNOWN):
            here = arrived[o, CAP * t : CAP * (t + 1)]
            wide[CAP * o : CAP * (o + 1), EXC * t : EXC * (t + 1), :] = here.astype(f32)
    packed[...] = wide[...].astype(bf16)
    lists.wait()

    for g in range(NB // GROUP):
        copies[g].wait()
        for j in range(GROUP):
            i = g * GROUP + j
            row = jnp.concatenate([packed[slots[s, i]] for s in range(L)], axis=1)
            tile = tiles[i].reshape(L * B, B)
            term = jnp.dot(row, tile, preferred_element_type=f32)
            for t in range(KNOWN):
                total[t, EXC * i : EXC * (i + 1), :] = term[EXC * t : EXC * (t + 1)]

    for y in range(4):
        for x in range(4):
            out[4 * y + x] = total[y % KNOWN, PART * x : PART * (x + 1), :].astype(bf16)


def add_terms(terms, out):
    total = terms[0].astype(f32)
    for k in range(1, LANES):
        total = total + terms[k].astype(f32)
    for x in range(4):
        out[x] = total


def solve(driven, diag, solved):
    for i in range(NB):
        row = driven[EXC * i : EXC * (i + 1), :].astype(bf16)
        solved[i] = jnp.dot(row, diag[i], preferred_element_type=f32)


def pick(asked, solved, send):
    for r in range(ROWS):
        for p in range(CAP):
            send[r, p] = solved[asked[r, p]].astype(bf16)


def first_step(asked, total, excite, diag, item, send, driven, solved):
    driven[...] = excite[0] - total[...]
    item[...] = driven[...].astype(bf16)
    solve(driven, diag, solved)
    pick(asked, solved, send)


def tile_terms(slots, tiles, arrived, total):
    for i in range(NB):
        row = jnp.concatenate([arrived[slots[s, i]] for s in range(L)], axis=1)
        tile = tiles[i].reshape(L * B, B)
        total[EXC * i : EXC * (i + 1), :] = jnp.dot(row, tile, preferred_element_type=f32)


def second_step(asked, total, came, h2, excite, diag, item, send, driven, solved):
    me = lax.axis_index("delay")
    value = total[...] + came[...]
    driven[...] = excite[1] - value

    @pl.when(me == 0)
    def _():
        item[...] = driven[...].astype(bf16).astype(f32)
        solve(driven, diag, solved)
        pick(asked, solved, send)

    @pl.when(me == 1)
    def _():
        item[...] = value

    @pl.when(me > 1)
    def _():
        for i in range(NB):
            item[EXC * i : EXC * (i + 1), :] = h2[i].astype(f32)


def third_step(asked, total, came, first, excite, diag, item, send, driven, solved):
    me = lax.axis_index("delay")
    other = jnp.where(me == 2, first[...].astype(f32), came[...])
    driven[...] = jnp.where(me == 0, excite[2] - (total[...] + came[...]), other)
    item[...] = driven[...].astype(bf16)

    @pl.when(me < KNOWN)
    def _():
        solve(driven, diag, solved)

    @pl.when(me >= KNOWN)
    def _():
        for i in range(NB):
            solved[i] = driven[EXC * i : EXC * (i + 1), :]

    pick(asked, solved, send)


def fourth_step(slots, tiles, arrived, item, out, total):
    tile_terms(slots, tiles, arrived, total)
    for k in range(LANES):
        mine = slice(SHARE * k, SHARE * (k + 1))
        out[k, :SHARE] = total[mine, :].astype(bf16)
        out[k, SHARE:] = item[mine, :]


def share_driven(parts, excite, out):
    total = parts[0, :SHARE].astype(f32)
    for k in range(1, LANES):
        total = total + parts[k, :SHARE].astype(f32)
    start = pl.multiple_of(lax.axis_index("delay") * SHARE, SHARE)
    last = (excite[STEPS - 1, pl.ds(start, SHARE), :] - total).astype(bf16)
    for k in range(LANES):
        for t in range(STEPS - 1):
            out[k, SHARE * t : SHARE * (t + 1)] = parts[STEPS - 2 - t, SHARE:]
        out[k, SHARE * (STEPS - 1) :] = last


def last_solve(driven, diag, out):
    each = SHARE // EXC
    for i in range(NB):
        value = jnp.dot(driven[i // each], diag[i], preferred_element_type=f32)
        for t in range(STEPS):
            at = SHARE * t + EXC * (i % each)
            out[t, i] = value[at : at + EXC]


def shifted(array, axis, by):
    peers = lax.axis_size(axis)
    return lax.ppermute(array, axis, [(i, i + by) for i in range(peers - by)])


def exchange(array, axis, groups=None):
    return lax.all_to_all(array, axis, split_axis=0, concat_axis=0, tiled=True, axis_index_groups=groups)


def body(retarded_tiles, wanted_blocks, tile_slots, diag_inverse, excitation, history_init):
    sds = jax.ShapeDtypeStruct
    stored = retarded_tiles[0]
    slots = tile_slots[0].T
    excite = excitation.reshape(STEPS, FLAT, B)

    asked = exchange(wanted_blocks[0, 0], "rows")
    h0 = history_init[0]
    later = []
    for t in range(1, KNOWN):
        later.append(shifted(h0, "delay", t))

    picked = call(
        pick_initial,
        sds((ROWS, KNOWN * CAP, EXC, B), bf16),
        [pltpu.VMEM(h0.shape, bf16), pltpu.SemaphoreType.DMA],
        (asked, h0, *later),
        (0,),
        (1,),
    )
    arrived = exchange(picked, "rows")
    wide = (TAKEN, EXC * STEPS, B)
    terms, tiles = call(
        initial_terms,
        (sds((LANES, PART, B), bf16), sds(stored.shape, bf16)),
        [
            pltpu.SMEM(slots.shape, jnp.int32),
            pltpu.VMEM(wide, f32),
            pltpu.VMEM(wide, bf16),
            pltpu.VMEM((KNOWN, FLAT, B), f32),
            pltpu.SemaphoreType.DMA,
            pltpu.SemaphoreType.DMA((NB // GROUP,)),
        ],
        (slots, stored, arrived),
        (),
        (0, 1),
    )
    terms = exchange(terms, "delay")
    part = call(add_terms, sds((4, PART, B), f32), [], (terms,), ())
    along_x = [[4 * y + x for x in range(4)] for y in range(4)]
    whole = exchange(part, "delay", along_x).reshape(FLAT, B)

    flat = pltpu.VMEM((FLAT, B), f32)
    block = pltpu.VMEM((NB, EXC, B), f32)
    send_shape = sds((ROWS, CAP, EXC, B), bf16)

    came = lax.ppermute(whole, "delay", [(4, 0), (9, 1)])
    item0, send = call(
        first_step,
        (sds((FLAT, B), bf16), send_shape),
        [flat, block],
        (asked, whole, excite, diag_inverse),
        (0,),
    )
    arrived = exchange(send, "rows").reshape(TAKEN, EXC, B)
    total = call(tile_terms, sds((FLAT, B), f32), [], (slots, tiles, arrived), (0,))

    item1, send = call(
        second_step,
        (sds((FLAT, B), f32), send_shape),
        [flat, block],
        (asked, total, came, later[1], excite, diag_inverse),
        (0,),
    )
    came = lax.ppermute(item1, "delay", [(0, 1), (1, 0)] + [(k, k + 1) for k in range(2, LANES - 1)])
    arrived = exchange(send, "rows").reshape(TAKEN, EXC, B)
    total = call(tile_terms, sds((FLAT, B), f32), [], (slots, tiles, arrived), (0,))

    item2, send = call(
        third_step,
        (sds((FLAT, B), bf16), send_shape),
        [flat, block],
        (asked, total, came, item0, excite, diag_inverse),
        (0,),
    )
    arrived = exchange(send, "rows").reshape(TAKEN, EXC, B)
    parts = call(
        fourth_step, sds((LANES, 2 * SHARE, B), bf16), [flat], (slots, tiles, arrived, item2), (0,)
    )
    parts = exchange(parts, "delay")
    shares = call(share_driven, sds((LANES, STEPS * SHARE, B), bf16), [], (parts, excite), ())
    driven = exchange(shares, "delay")
    return call(last_solve, sds((STEPS, NB, EXC, B), f32), [], (driven, diag_inverse), ())


def solution(mesh):
    return jax.shard_map(
        body,
        mesh=mesh,
        in_specs=(
            P("delay", "rows", None, None, None),
            P("delay", "rows", None, None),
            P("delay", "rows", None),
            P("rows", None, None),
            P(None, "rows", None, None),
            P("delay", "rows", None, None),
        ),
        out_specs=P(None, "rows", None, None),
        check_vma=False,
    )
```

```python
import jax
import jax.numpy as jnp
from jax import lax
from jax.experimental import pallas as pl
from jax.experimental.pallas import tpu as pltpu
from jax.sharding import PartitionSpec as P


STEPS = 4
LANES = 16
ROWS = 16
CAP = 8
NB = 64
EXC = 4
B = 128
L = 4
TAKEN = ROWS * CAP
FLAT = NB * EXC
KNOWN = 3
GIVERS = (4, 9)
SHARE = FLAT // LANES
GROUP = 16

bf16 = jnp.bfloat16
f32 = jnp.float32
VMEM = pl.BlockSpec(memory_space=pltpu.VMEM)
SMEM = pl.BlockSpec(memory_space=pltpu.SMEM)
HBM = pl.BlockSpec(memory_space=pltpu.HBM)
LIMIT = 16 * 1024 * 1024


def call(kernel, out_shape, scratch, operands, in_smem, in_place=(), out_in_place=False):
    specs = [SMEM if i in in_smem else HBM if i in in_place else VMEM for i in range(len(operands))]
    many = isinstance(out_shape, (tuple, list))
    operands = [pltpu.with_memory_space_constraint(x, pltpu.HBM) if i in in_place else x for i, x in enumerate(operands)]
    return pl.pallas_call(
        kernel,
        out_shape=out_shape,
        in_specs=specs,
        out_specs=[VMEM] * len(out_shape) if many else (HBM if out_in_place else VMEM),
        scratch_shapes=scratch,
        compiler_params=pltpu.CompilerParams(vmem_limit_bytes=LIMIT),
    )(*operands)


def pick_initial(asked, stored, tiles, h1, h2, out, h0, sem):
    copy = pltpu.make_async_copy(stored, h0, sem)
    copy.start()
    for r in range(ROWS):
        for p in range(CAP):
            at = asked[r, p]
            out[r, CAP + p] = h1[at]
            out[r, 2 * CAP + p] = h2[at]
    copy.wait()
    for r in range(ROWS):
        for p in range(CAP):
            out[r, p] = h0[asked[r, p]]


def initial_terms(slots, tiles, arrived, out, wide, packed, total):
    for o in range(ROWS):
        for t in range(KNOWN):
            here = arrived[o, CAP * t : CAP * (t + 1)]
            wide[CAP * o : CAP * (o + 1), EXC * t : EXC * (t + 1), :] = here.astype(f32)
    packed[...] = wide[...].astype(bf16)
    for i in range(NB):
        row = jnp.concatenate([packed[slots[s, i]] for s in range(L)], axis=1)
        tile = tiles[i].reshape(L * B, B)
        term = jnp.dot(row, tile, preferred_element_type=f32)
        for t in range(KNOWN):
            total[t, EXC * i : EXC * (i + 1), :] = term[EXC * t : EXC * (t + 1)]

    for y in range(4):
        out[y] = total[y % KNOWN].astype(bf16)


def add_terms(terms, out):
    total = sum(terms[y].astype(f32) for y in range(4)).astype(bf16)
    for x in range(4):
        out[x] = total


def solve(driven, diag, solved):
    for i in range(NB):
        row = driven[EXC * i : EXC * (i + 1), :].astype(bf16)
        solved[i] = jnp.dot(row, diag[i], preferred_element_type=f32)


def pick(fetch, asked, solved, send):
    fetch.wait()
    for r in range(ROWS):
        for p in range(CAP):
            send[r, p] = solved[asked[r, p]].astype(bf16)


def older(h2, item):
    for i in range(NB):
        item[EXC * i : EXC * (i + 1), :] = h2[i].astype(f32)


def first_step(listed, terms, h2, excite, diag, moved, item, send, driven, solved, asked, sem):
    fetch = pltpu.make_async_copy(listed, asked, sem)
    fetch.start()
    me = lax.axis_index("delay")
    whole = sum(terms[x].astype(f32) for x in range(4))
    driven[...] = excite[0] - whole
    gives = (me == GIVERS[0]) | (me == GIVERS[1])

    @pl.when(gives)
    def _():
        moved[...] = whole

    @pl.when(jnp.logical_not(gives))
    def _():
        older(h2, moved)

    item[...] = driven[...].astype(bf16)
    solve(driven, diag, solved)
    pick(fetch, asked, solved, send)


def tile_terms(slots, tiles, arrived, total):
    for i in range(NB):
        row = jnp.concatenate([arrived[slots[s, i]] for s in range(L)], axis=1)
        tile = tiles[i].reshape(L * B, B)
        total[EXC * i : EXC * (i + 1), :] = jnp.dot(row, tile, preferred_element_type=f32)


def second_step(listed, total, came, h2, excite, diag, item, send, driven, solved, asked, sem):
    fetch = pltpu.make_async_copy(listed, asked, sem)
    fetch.start()
    me = lax.axis_index("delay")
    value = total[...] + came[...]
    driven[...] = excite[1] - value

    @pl.when(me == 0)
    def _():
        item[...] = driven[...].astype(bf16).astype(f32)
        solve(driven, diag, solved)
        pick(fetch, asked, solved, send)

    @pl.when(me != 0)
    def _():
        fetch.wait()

    @pl.when(me == 1)
    def _():
        item[...] = value

    @pl.when(me > 1)
    def _():
        older(h2, item)


def third_step(listed, total, came, before, first, excite, diag, item, send, driven, solved, asked, sem):
    fetch = pltpu.make_async_copy(listed, asked, sem)
    fetch.start()
    me = lax.axis_index("delay")
    late = (me == 1) | (me == GIVERS[0] + 1) | (me == GIVERS[1] + 1)
    other = jnp.where(me == 2, first[...].astype(f32), jnp.where(late, came[...], before[...]))
    driven[...] = jnp.where(me == 0, excite[2] - (total[...] + came[...]), other)
    item[...] = driven[...].astype(bf16)

    @pl.when(me < KNOWN)
    def _():
        solve(driven, diag, solved)

    @pl.when(me >= KNOWN)
    def _():
        for i in range(NB):
            solved[i] = driven[EXC * i : EXC * (i + 1), :]

    pick(fetch, asked, solved, send)


def fourth_step(slots, tiles, arrived, item, out, total):
    tile_terms(slots, tiles, arrived, total)
    for k in range(LANES):
        mine = slice(SHARE * k, SHARE * (k + 1))
        out[k, :SHARE] = total[mine, :].astype(bf16)
        out[k, SHARE:] = item[mine, :]


def share_driven(parts, excite, out):
    total = parts[0, :SHARE].astype(f32)
    for k in range(1, LANES):
        total = total + parts[k, :SHARE].astype(f32)
    start = pl.multiple_of(lax.axis_index("delay") * SHARE, SHARE)
    last = (excite[STEPS - 1, pl.ds(start, SHARE), :] - total).astype(bf16)
    for k in range(LANES):
        for t in range(STEPS - 1):
            out[k, SHARE * t : SHARE * (t + 1)] = parts[STEPS - 2 - t, SHARE:]
        out[k, SHARE * (STEPS - 1) :] = last


def last_solve(driven, diag, stored, out, sems):
    each = SHARE // EXC
    copies = []
    for i in range(NB):
        value = jnp.dot(driven[i // each], diag[i], preferred_element_type=f32)
        for t in range(STEPS):
            at = SHARE * t + EXC * (i % each)
            out[t, i] = value[at : at + EXC]
        if i % GROUP == GROUP - 1:
            for t in range(STEPS):
                part = (t, pl.ds(i - GROUP + 1, GROUP))
                copies.append(pltpu.make_async_copy(out.at[part], stored.at[part], sems.at[len(copies)]))
                copies[-1].start()
    for copy in copies:
        copy.wait()


def shifted(array, axis, by):
    peers = lax.axis_size(axis)
    return lax.ppermute(array, axis, [(i, i + by) for i in range(peers - by)])


def exchange(array, axis, groups=None):
    return lax.all_to_all(array, axis, split_axis=0, concat_axis=0, tiled=True, axis_index_groups=groups)


def body(retarded_tiles, wanted_blocks, tile_slots, diag_inverse, excitation, history_init):
    sds = jax.ShapeDtypeStruct
    tiles = retarded_tiles[0]
    slots = tile_slots[0].T
    excite = excitation.reshape(STEPS, FLAT, B)

    asked = exchange(wanted_blocks[0, 0], "rows")
    h0 = history_init[0]
    later = []
    for t in range(1, KNOWN):
        later.append(shifted(h0, "delay", t))

    picked = call(
        pick_initial,
        sds((ROWS, KNOWN * CAP, EXC, B), bf16),
        [pltpu.VMEM(h0.shape, bf16), pltpu.SemaphoreType.DMA],
        (asked, h0, tiles, *later),
        (0,),
        (1, 2),
    )
    arrived = exchange(picked, "rows")
    wide = (TAKEN, EXC * STEPS, B)
    terms = call(
        initial_terms,
        sds((4, FLAT, B), bf16),
        [pltpu.VMEM(wide, f32), pltpu.VMEM(wide, bf16), pltpu.VMEM((KNOWN, FLAT, B), f32)],
        (slots, tiles, arrived),
        (0,),
    )
    along_x = [[4 * y + x for x in range(4)] for y in range(4)]
    along_y = [[4 * y + x for y in range(4)] for x in range(4)]
    terms = exchange(terms, "delay", along_y)
    terms = call(add_terms, sds((4, FLAT, B), bf16), [], (terms,), ())
    terms = exchange(terms, "delay", along_x)

    flat = pltpu.VMEM((FLAT, B), f32)
    block = pltpu.VMEM((NB, EXC, B), f32)
    work = [flat, block, pltpu.SMEM((ROWS, CAP), jnp.int32), pltpu.SemaphoreType.DMA]
    send_shape = sds((ROWS, CAP, EXC, B), bf16)

    moved, item0, send = call(
        first_step,
        (sds((FLAT, B), f32), sds((FLAT, B), bf16), send_shape),
        work,
        (asked, terms, later[1], excite, diag_inverse),
        (),
    )
    steps = [(k, k + 1) for k in range(2, LANES - 1)]
    pairs = [(k, j) for k, j in steps if k not in GIVERS]
    before = lax.ppermute(moved, "delay", [(GIVERS[0], 0), (GIVERS[1], 1)] + pairs)
    arrived = exchange(send, "rows").reshape(TAKEN, EXC, B)
    total = call(tile_terms, sds((FLAT, B), f32), [], (slots, tiles, arrived), (0,))

    item1, send = call(
        second_step,
        (sds((FLAT, B), f32), send_shape),
        work,
        (asked, total, before, later[1], excite, diag_inverse),
        (),
    )
    came = lax.ppermute(item1, "delay", [(0, 1), (1, 0)] + [(k, j) for k, j in steps if k in GIVERS])
    arrived = exchange(send, "rows").reshape(TAKEN, EXC, B)
    total = call(tile_terms, sds((FLAT, B), f32), [], (slots, tiles, arrived), (0,))

    item2, send = call(
        third_step,
        (sds((FLAT, B), bf16), send_shape),
        work,
        (asked, total, came, before, item0, excite, diag_inverse),
        (),
    )
    arrived = exchange(send, "rows").reshape(TAKEN, EXC, B)
    parts = call(
        fourth_step, sds((LANES, 2 * SHARE, B), bf16), [flat], (slots, tiles, arrived, item2), (0,)
    )
    parts = exchange(parts, "delay")
    shares = call(share_driven, sds((LANES, STEPS * SHARE, B), bf16), [], (parts, excite), ())
    driven = exchange(shares, "delay")
    final = (STEPS, NB, EXC, B)
    return call(
        last_solve,
        sds(final, f32),
        [pltpu.VMEM(final, f32), pltpu.SemaphoreType.DMA((STEPS * NB // GROUP,))],
        (driven, diag_inverse),
        (),
        out_in_place=True,
    )


def solution(mesh):
    return jax.shard_map(
        body,
        mesh=mesh,
        in_specs=(
            P("delay", "rows", None, None, None),
            P("delay", "rows", None, None),
            P("delay", "rows", None),
            P("rows", None, None),
            P(None, "rows", None, None),
            P("delay", "rows", None, None),
        ),
        out_specs=P(None, "rows", None, None),
        check_vma=False,
    )
```

```python
import jax
import jax.numpy as jnp
from jax import lax
from jax.experimental import pallas as pl
from jax.experimental.pallas import tpu as pltpu
from jax.sharding import PartitionSpec as P


STEPS = 4
LANES = 16
ROWS = 16
CAP = 8
NB = 64
EXC = 4
B = 128
L = 4
TAKEN = ROWS * CAP
FLAT = NB * EXC
KNOWN = 3
GIVERS = (4, 9)
SHARE = FLAT // LANES
GROUP = 16

bf16 = jnp.bfloat16
f32 = jnp.float32
VMEM = pl.BlockSpec(memory_space=pltpu.VMEM)
SMEM = pl.BlockSpec(memory_space=pltpu.SMEM)
HBM = pl.BlockSpec(memory_space=pltpu.HBM)
LIMIT = 16 * 1024 * 1024


def call(kernel, out_shape, scratch, operands, in_smem, in_place=(), out_in_place=False):
    specs = [SMEM if i in in_smem else HBM if i in in_place else VMEM for i in range(len(operands))]
    many = isinstance(out_shape, (tuple, list))
    operands = [pltpu.with_memory_space_constraint(x, pltpu.HBM) if i in in_place else x for i, x in enumerate(operands)]
    return pl.pallas_call(
        kernel,
        out_shape=out_shape,
        in_specs=specs,
        out_specs=[VMEM] * len(out_shape) if many else (HBM if out_in_place else VMEM),
        scratch_shapes=scratch,
        compiler_params=pltpu.CompilerParams(vmem_limit_bytes=LIMIT),
    )(*operands)


def pick_initial(listed, stored, tiles, h1, h2, out, h0, asked, sem, list_sem):
    copy = pltpu.make_async_copy(stored, h0, sem)
    copy.start()
    fetch = pltpu.make_async_copy(listed, asked, list_sem)
    fetch.start()
    fetch.wait()
    for r in range(ROWS):
        for p in range(CAP):
            at = asked[r, p]
            out[r, CAP + p] = h1[at]
            out[r, 2 * CAP + p] = h2[at]
    copy.wait()
    for r in range(ROWS):
        for p in range(CAP):
            out[r, p] = h0[asked[r, p]]


def initial_terms(slots, tiles, arrived, out, wide, packed, total):
    for o in range(ROWS):
        for t in range(KNOWN):
            here = arrived[o, CAP * t : CAP * (t + 1)]
            wide[CAP * o : CAP * (o + 1), EXC * t : EXC * (t + 1), :] = here.astype(f32)
    packed[...] = wide[...].astype(bf16)
    for i in range(NB):
        row = jnp.concatenate([packed[slots[s, i]] for s in range(L)], axis=1)
        tile = tiles[i].reshape(L * B, B)
        term = jnp.dot(row, tile, preferred_element_type=f32)
        for t in range(KNOWN):
            total[t, EXC * i : EXC * (i + 1), :] = term[EXC * t : EXC * (t + 1)]

    for y in range(4):
        out[y] = total[y % KNOWN].astype(bf16)


def add_terms(terms, out):
    total = sum(terms[y].astype(f32) for y in range(4)).astype(bf16)
    for x in range(4):
        out[x] = total


def solve(driven, diag, solved):
    for i in range(NB):
        row = driven[EXC * i : EXC * (i + 1), :].astype(bf16)
        solved[i] = jnp.dot(row, diag[i], preferred_element_type=f32)


def pick(fetch, asked, solved, send):
    fetch.wait()
    for r in range(ROWS):
        for p in range(CAP):
            send[r, p] = solved[asked[r, p]].astype(bf16)


def older(h2, item):
    for i in range(NB):
        item[EXC * i : EXC * (i + 1), :] = h2[i].astype(f32)


def first_step(listed, terms, h2, excite, diag, moved, item, send, driven, solved, asked, sem):
    fetch = pltpu.make_async_copy(listed, asked, sem)
    fetch.start()
    me = lax.axis_index("delay")
    whole = sum(terms[x].astype(f32) for x in range(4))
    driven[...] = excite[0] - whole
    gives = (me == GIVERS[0]) | (me == GIVERS[1])

    @pl.when(gives)
    def _():
        moved[...] = whole

    @pl.when(jnp.logical_not(gives))
    def _():
        older(h2, moved)

    item[...] = driven[...].astype(bf16)
    solve(driven, diag, solved)
    pick(fetch, asked, solved, send)


def tile_terms(slots, tiles, arrived, total):
    for i in range(NB):
        row = jnp.concatenate([arrived[slots[s, i]] for s in range(L)], axis=1)
        tile = tiles[i].reshape(L * B, B)
        total[EXC * i : EXC * (i + 1), :] = jnp.dot(row, tile, preferred_element_type=f32)


def second_step(listed, total, came, h2, excite, diag, item, send, driven, solved, asked, sem):
    fetch = pltpu.make_async_copy(listed, asked, sem)
    fetch.start()
    me = lax.axis_index("delay")
    value = total[...] + came[...]
    driven[...] = excite[1] - value

    @pl.when(me == 0)
    def _():
        item[...] = driven[...].astype(bf16).astype(f32)
        solve(driven, diag, solved)
        pick(fetch, asked, solved, send)

    @pl.when(me != 0)
    def _():
        fetch.wait()

    @pl.when(me == 1)
    def _():
        item[...] = value

    @pl.when(me > 1)
    def _():
        older(h2, item)


def third_step(listed, total, came, before, first, excite, diag, item, send, driven, solved, asked, sem):
    fetch = pltpu.make_async_copy(listed, asked, sem)
    fetch.start()
    me = lax.axis_index("delay")
    late = (me == 1) | (me == GIVERS[0] + 1) | (me == GIVERS[1] + 1)
    other = jnp.where(me == 2, first[...].astype(f32), jnp.where(late, came[...], before[...]))
    driven[...] = jnp.where(me == 0, excite[2] - (total[...] + came[...]), other)
    item[...] = driven[...].astype(bf16)

    @pl.when(me < KNOWN)
    def _():
        solve(driven, diag, solved)

    @pl.when(me >= KNOWN)
    def _():
        for i in range(NB):
            solved[i] = driven[EXC * i : EXC * (i + 1), :]

    pick(fetch, asked, solved, send)


def fourth_step(slots, tiles, arrived, item, out, total):
    tile_terms(slots, tiles, arrived, total)
    for k in range(LANES):
        mine = slice(SHARE * k, SHARE * (k + 1))
        out[k, :SHARE] = total[mine, :].astype(bf16)
        out[k, SHARE:] = item[mine, :]


def share_driven(parts, excite, out, rows):
    total = parts[0, :SHARE].astype(f32)
    for k in range(1, LANES):
        total = total + parts[k, :SHARE].astype(f32)
    start = pl.multiple_of(lax.axis_index("delay") * SHARE, SHARE)
    last = excite[STEPS - 1, pl.ds(start, SHARE), :] - total
    values = [parts[STEPS - 2 - t, SHARE:].astype(f32) for t in range(STEPS - 1)] + [last]
    for t, value in enumerate(values):
        for b in range(SHARE // EXC):
            at = EXC * (STEPS * b + t)
            rows[at : at + EXC] = value[EXC * b : EXC * (b + 1)]
    both = rows[...].astype(bf16)
    for k in range(LANES):
        out[k] = both


def last_solve(driven, diag, stored, out, sems):
    each = SHARE // EXC
    copies = []
    for i in range(NB):
        mine = slice(EXC * STEPS * (i % each), EXC * STEPS * (i % each + 1))
        value = jnp.dot(driven[i // each, mine], diag[i], preferred_element_type=f32)
        for t in range(STEPS):
            out[t, i] = value[EXC * t : EXC * (t + 1)]
        if i % GROUP == GROUP - 1:
            part = (slice(None), pl.ds(i - GROUP + 1, GROUP))
            copies.append(pltpu.make_async_copy(out.at[part], stored.at[part], sems.at[len(copies)]))
            copies[-1].start()
    for copy in copies:
        copy.wait()


def shifted(array, axis, by):
    peers = lax.axis_size(axis)
    return lax.ppermute(array, axis, [(i, i + by) for i in range(peers - by)])


def exchange(array, axis, groups=None):
    return lax.all_to_all(array, axis, split_axis=0, concat_axis=0, tiled=True, axis_index_groups=groups)


def body(retarded_tiles, wanted_blocks, tile_slots, diag_inverse, excitation, history_init):
    sds = jax.ShapeDtypeStruct
    tiles = retarded_tiles[0]
    slots = tile_slots[0].T
    excite = excitation.reshape(STEPS, FLAT, B)

    asked = exchange(wanted_blocks[0, 0], "rows")
    h0 = history_init[0]
    later = []
    for t in range(1, KNOWN):
        later.append(shifted(h0, "delay", t))

    picked = call(
        pick_initial,
        sds((ROWS, KNOWN * CAP, EXC, B), bf16),
        [
            pltpu.VMEM(h0.shape, bf16),
            pltpu.SMEM((ROWS, CAP), jnp.int32),
            pltpu.SemaphoreType.DMA,
            pltpu.SemaphoreType.DMA,
        ],
        (asked, h0, tiles, *later),
        (),
        (1, 2),
    )
    arrived = exchange(picked, "rows")
    wide = (TAKEN, EXC * STEPS, B)
    terms = call(
        initial_terms,
        sds((4, FLAT, B), bf16),
        [pltpu.VMEM(wide, f32), pltpu.VMEM(wide, bf16), pltpu.VMEM((KNOWN, FLAT, B), f32)],
        (slots, tiles, arrived),
        (0,),
    )
    along_x = [[4 * y + x for x in range(4)] for y in range(4)]
    along_y = [[4 * y + x for y in range(4)] for x in range(4)]
    terms = exchange(terms, "delay", along_y)
    terms = call(add_terms, sds((4, FLAT, B), bf16), [], (terms,), ())
    terms = exchange(terms, "delay", along_x)

    flat = pltpu.VMEM((FLAT, B), f32)
    block = pltpu.VMEM((NB, EXC, B), f32)
    work = [flat, block, pltpu.SMEM((ROWS, CAP), jnp.int32), pltpu.SemaphoreType.DMA]
    send_shape = sds((ROWS, CAP, EXC, B), bf16)

    moved, item0, send = call(
        first_step,
        (sds((FLAT, B), f32), sds((FLAT, B), bf16), send_shape),
        work,
        (asked, terms, later[1], excite, diag_inverse),
        (),
    )
    steps = [(k, k + 1) for k in range(2, LANES - 1)]
    pairs = [(k, j) for k, j in steps if k not in GIVERS]
    before = lax.ppermute(moved, "delay", [(GIVERS[0], 0), (GIVERS[1], 1)] + pairs)
    arrived = exchange(send, "rows").reshape(TAKEN, EXC, B)
    total = call(tile_terms, sds((FLAT, B), f32), [], (slots, tiles, arrived), (0,))

    item1, send = call(
        second_step,
        (sds((FLAT, B), f32), send_shape),
        work,
        (asked, total, before, later[1], excite, diag_inverse),
        (),
    )
    came = lax.ppermute(item1, "delay", [(0, 1), (1, 0)] + [(k, j) for k, j in steps if k in GIVERS])
    arrived = exchange(send, "rows").reshape(TAKEN, EXC, B)
    total = call(tile_terms, sds((FLAT, B), f32), [], (slots, tiles, arrived), (0,))

    item2, send = call(
        third_step,
        (sds((FLAT, B), bf16), send_shape),
        work,
        (asked, total, came, before, item0, excite, diag_inverse),
        (),
    )
    arrived = exchange(send, "rows").reshape(TAKEN, EXC, B)
    parts = call(
        fourth_step, sds((LANES, 2 * SHARE, B), bf16), [flat], (slots, tiles, arrived, item2), (0,)
    )
    parts = exchange(parts, "delay")
    shares = call(
        share_driven, sds((LANES, STEPS * SHARE, B), bf16), [pltpu.VMEM((STEPS * SHARE, B), f32)], (parts, excite), ()
    )
    driven = exchange(shares, "delay")
    final = (STEPS, NB, EXC, B)
    return call(
        last_solve,
        sds(final, f32),
        [pltpu.VMEM(final, f32), pltpu.SemaphoreType.DMA((NB // GROUP,))],
        (driven, diag_inverse),
        (),
        out_in_place=True,
    )


def solution(mesh):
    return jax.shard_map(
        body,
        mesh=mesh,
        in_specs=(
            P("delay", "rows", None, None, None),
            P("delay", "rows", None, None),
            P("delay", "rows", None),
            P("rows", None, None),
            P(None, "rows", None, None),
            P("delay", "rows", None, None),
        ),
        out_specs=P(None, "rows", None, None),
        check_vma=False,
    )
```

```python
import functools

import jax
import jax.numpy as jnp
from jax import lax
from jax.experimental import pallas as pl
from jax.experimental.pallas import tpu as pltpu
from jax.sharding import PartitionSpec as P


STEPS = 4
LANES = 16
ROWS = 16
CAP = 8
NB = 64
EXC = 4
B = 128
L = 4
TAKEN = ROWS * CAP
FLAT = NB * EXC
KNOWN = 3
GIVERS = (4, 9)
SHARE = FLAT // LANES
GROUP = 16

bf16 = jnp.bfloat16
f32 = jnp.float32
VMEM = pl.BlockSpec(memory_space=pltpu.VMEM)
SMEM = pl.BlockSpec(memory_space=pltpu.SMEM)
HBM = pl.BlockSpec(memory_space=pltpu.HBM)
LIMIT = 16 * 1024 * 1024


def call(kernel, out_shape, scratch, operands, in_smem, in_place=(), out_in_place=False):
    specs = [SMEM if i in in_smem else HBM if i in in_place else VMEM for i in range(len(operands))]
    many = isinstance(out_shape, (tuple, list))
    operands = [pltpu.with_memory_space_constraint(x, pltpu.HBM) if i in in_place else x for i, x in enumerate(operands)]
    return pl.pallas_call(
        kernel,
        out_shape=out_shape,
        in_specs=specs,
        out_specs=[VMEM] * len(out_shape) if many else (HBM if out_in_place else VMEM),
        scratch_shapes=scratch,
        compiler_params=pltpu.CompilerParams(vmem_limit_bytes=LIMIT),
    )(*operands)


def pick_initial(listed, stored, tiles, h1, h2, out, h0, asked, sem, list_sem):
    copy = pltpu.make_async_copy(stored, h0, sem)
    copy.start()
    fetch = pltpu.make_async_copy(listed, asked, list_sem)
    fetch.start()
    fetch.wait()
    for r in range(ROWS):
        for p in range(CAP):
            at = asked[r, p]
            out[r, CAP + p] = h1[at]
            out[r, 2 * CAP + p] = h2[at]
    copy.wait()
    for r in range(ROWS):
        for p in range(CAP):
            out[r, p] = h0[asked[r, p]]


def initial_terms(slots, tiles, arrived, out, wide, packed, total):
    for o in range(ROWS):
        for t in range(KNOWN):
            here = arrived[o, CAP * t : CAP * (t + 1)]
            wide[CAP * o : CAP * (o + 1), EXC * t : EXC * (t + 1), :] = here.astype(f32)
    packed[...] = wide[...].astype(bf16)
    for i in range(NB):
        row = jnp.concatenate([packed[slots[s, i]] for s in range(L)], axis=1)
        tile = tiles[i].reshape(L * B, B)
        term = jnp.dot(row, tile, preferred_element_type=f32)
        for t in range(KNOWN):
            total[t, EXC * i : EXC * (i + 1), :] = term[EXC * t : EXC * (t + 1)]

    for y in range(4):
        out[y] = total[y % KNOWN].astype(bf16)


def add_terms(terms, out):
    total = sum(terms[y].astype(f32) for y in range(4)).astype(bf16)
    for x in range(4):
        out[x] = total


def solve(driven, diag, solved):
    for i in range(NB):
        row = driven[EXC * i : EXC * (i + 1), :].astype(bf16)
        solved[i] = jnp.dot(row, diag[i], preferred_element_type=f32)


def pick(fetch, asked, solved, send):
    fetch.wait()
    for r in range(ROWS):
        for p in range(CAP):
            send[r, p] = solved[asked[r, p]].astype(bf16)


def older(h2, item):
    for i in range(NB):
        item[EXC * i : EXC * (i + 1), :] = h2[i].astype(f32)


def first_step(listed, terms, h2, excite, diag, moved, item, send, driven, solved, asked, sem):
    fetch = pltpu.make_async_copy(listed, asked, sem)
    fetch.start()
    me = lax.axis_index("delay")
    whole = sum(terms[x].astype(f32) for x in range(4))
    driven[...] = excite[0] - whole
    gives = (me == GIVERS[0]) | (me == GIVERS[1])

    @pl.when(gives)
    def _():
        moved[...] = whole

    @pl.when(jnp.logical_not(gives))
    def _():
        older(h2, moved)

    item[...] = driven[...].astype(bf16)

    @pl.when(me < 2)
    def _():
        solve(driven, diag, solved)
        pick(fetch, asked, solved, send)

    @pl.when(me >= 2)
    def _():
        fetch.wait()


def tile_terms(slots, tiles, arrived, total):
    for i in range(NB):
        row = jnp.concatenate([arrived[slots[s, i]] for s in range(L)], axis=1)
        tile = tiles[i].reshape(L * B, B)
        total[EXC * i : EXC * (i + 1), :] = jnp.dot(row, tile, preferred_element_type=f32)


def tile_terms_below(lanes, slots, tiles, arrived, total):
    @pl.when(lax.axis_index("delay") < lanes)
    def _():
        tile_terms(slots, tiles, arrived, total)


def second_step(listed, total, came, h2, excite, diag, item, send, driven, solved, asked, sem):
    fetch = pltpu.make_async_copy(listed, asked, sem)
    fetch.start()
    me = lax.axis_index("delay")
    value = total[...] + came[...]
    driven[...] = excite[1] - value

    @pl.when(me == 0)
    def _():
        item[...] = driven[...].astype(bf16).astype(f32)
        solve(driven, diag, solved)
        pick(fetch, asked, solved, send)

    @pl.when(me != 0)
    def _():
        fetch.wait()

    @pl.when(me == 1)
    def _():
        item[...] = value

    @pl.when(me > 1)
    def _():
        older(h2, item)


def third_step(listed, total, came, before, first, excite, diag, item, send, driven, solved, asked, sem):
    fetch = pltpu.make_async_copy(listed, asked, sem)
    fetch.start()
    me = lax.axis_index("delay")
    late = (me == 1) | (me == GIVERS[0] + 1) | (me == GIVERS[1] + 1)
    other = jnp.where(me == 2, first[...].astype(f32), jnp.where(late, came[...], before[...]))
    driven[...] = jnp.where(me == 0, excite[2] - (total[...] + came[...]), other)
    item[...] = driven[...].astype(bf16)

    @pl.when(me < KNOWN)
    def _():
        solve(driven, diag, solved)

    @pl.when(me >= KNOWN)
    def _():
        for i in range(NB):
            solved[i] = driven[EXC * i : EXC * (i + 1), :]

    pick(fetch, asked, solved, send)


def fourth_step(slots, tiles, arrived, item, out, total):
    tile_terms(slots, tiles, arrived, total)
    for k in range(LANES):
        mine = slice(SHARE * k, SHARE * (k + 1))
        out[k, :SHARE] = total[mine, :].astype(bf16)
        out[k, SHARE:] = item[mine, :]


def share_driven(parts, excite, out, rows):
    total = parts[0, :SHARE].astype(f32)
    for k in range(1, LANES):
        total = total + parts[k, :SHARE].astype(f32)
    start = pl.multiple_of(lax.axis_index("delay") * SHARE, SHARE)
    last = excite[STEPS - 1, pl.ds(start, SHARE), :] - total
    values = [parts[STEPS - 2 - t, SHARE:].astype(f32) for t in range(STEPS - 1)] + [last]
    for t, value in enumerate(values):
        for b in range(SHARE // EXC):
            at = EXC * (STEPS * b + t)
            rows[at : at + EXC] = value[EXC * b : EXC * (b + 1)]
    both = rows[...].astype(bf16)
    for k in range(LANES):
        out[k] = both


def last_solve(driven, diag, stored, out, sems):
    each = SHARE // EXC
    copies = []
    for i in range(NB):
        mine = slice(EXC * STEPS * (i % each), EXC * STEPS * (i % each + 1))
        value = jnp.dot(driven[i // each, mine], diag[i], preferred_element_type=f32)
        for t in range(STEPS):
            out[t, i] = value[EXC * t : EXC * (t + 1)]
        if i % GROUP == GROUP - 1:
            part = (slice(None), pl.ds(i - GROUP + 1, GROUP))
            copies.append(pltpu.make_async_copy(out.at[part], stored.at[part], sems.at[len(copies)]))
            copies[-1].start()
    for copy in copies:
        copy.wait()


def shifted(array, axis, by):
    peers = lax.axis_size(axis)
    return lax.ppermute(array, axis, [(i, i + by) for i in range(peers - by)])


def exchange(array, axis, groups=None):
    return lax.all_to_all(array, axis, split_axis=0, concat_axis=0, tiled=True, axis_index_groups=groups)


def body(retarded_tiles, wanted_blocks, tile_slots, diag_inverse, excitation, history_init):
    sds = jax.ShapeDtypeStruct
    tiles = retarded_tiles[0]
    slots = tile_slots[0].T
    excite = excitation.reshape(STEPS, FLAT, B)

    asked = exchange(wanted_blocks[0, 0], "rows")
    h0 = history_init[0]
    later = []
    for t in range(1, KNOWN):
        later.append(shifted(h0, "delay", t))

    picked = call(
        pick_initial,
        sds((ROWS, KNOWN * CAP, EXC, B), bf16),
        [
            pltpu.VMEM(h0.shape, bf16),
            pltpu.SMEM((ROWS, CAP), jnp.int32),
            pltpu.SemaphoreType.DMA,
            pltpu.SemaphoreType.DMA,
        ],
        (asked, h0, tiles, *later),
        (),
        (1, 2),
    )
    arrived = exchange(picked, "rows")
    wide = (TAKEN, EXC * STEPS, B)
    terms = call(
        initial_terms,
        sds((4, FLAT, B), bf16),
        [pltpu.VMEM(wide, f32), pltpu.VMEM(wide, bf16), pltpu.VMEM((KNOWN, FLAT, B), f32)],
        (slots, tiles, arrived),
        (0,),
    )
    along_x = [[4 * y + x for x in range(4)] for y in range(4)]
    along_y = [[4 * y + x for y in range(4)] for x in range(4)]
    terms = exchange(terms, "delay", along_y)
    terms = call(add_terms, sds((4, FLAT, B), bf16), [], (terms,), ())
    terms = exchange(terms, "delay", along_x)

    flat = pltpu.VMEM((FLAT, B), f32)
    block = pltpu.VMEM((NB, EXC, B), f32)
    work = [flat, block, pltpu.SMEM((ROWS, CAP), jnp.int32), pltpu.SemaphoreType.DMA]
    send_shape = sds((ROWS, CAP, EXC, B), bf16)

    moved, item0, send = call(
        first_step,
        (sds((FLAT, B), f32), sds((FLAT, B), bf16), send_shape),
        work,
        (asked, terms, later[1], excite, diag_inverse),
        (),
    )
    steps = [(k, k + 1) for k in range(2, LANES - 1)]
    pairs = [(k, j) for k, j in steps if k not in GIVERS]
    before = lax.ppermute(moved, "delay", [(GIVERS[0], 0), (GIVERS[1], 1)] + pairs)
    arrived = exchange(send, "rows").reshape(TAKEN, EXC, B)
    total = call(functools.partial(tile_terms_below, 2), sds((FLAT, B), f32), [], (slots, tiles, arrived), (0,))

    item1, send = call(
        second_step, (sds((FLAT, B), f32), send_shape), work, (asked, total, before, later[1], excite, diag_inverse), ()
    )
    came = lax.ppermute(item1, "delay", [(0, 1), (1, 0)] + [(k, j) for k, j in steps if k in GIVERS])
    arrived = exchange(send, "rows").reshape(TAKEN, EXC, B)
    total = call(functools.partial(tile_terms_below, 1), sds((FLAT, B), f32), [], (slots, tiles, arrived), (0,))

    item2, send = call(
        third_step,
        (sds((FLAT, B), bf16), send_shape),
        work,
        (asked, total, came, before, item0, excite, diag_inverse),
        (),
    )
    arrived = exchange(send, "rows").reshape(TAKEN, EXC, B)
    parts = call(fourth_step, sds((LANES, 2 * SHARE, B), bf16), [flat], (slots, tiles, arrived, item2), (0,))
    parts = exchange(parts, "delay")
    shares = call(
        share_driven, sds((LANES, STEPS * SHARE, B), bf16), [pltpu.VMEM((STEPS * SHARE, B), f32)], (parts, excite), ()
    )
    driven = exchange(shares, "delay")
    final = (STEPS, NB, EXC, B)
    return call(
        last_solve,
        sds(final, f32),
        [pltpu.VMEM(final, f32), pltpu.SemaphoreType.DMA((NB // GROUP,))],
        (driven, diag_inverse),
        (),
        out_in_place=True,
    )


def solution(mesh):
    return jax.shard_map(
        body,
        mesh=mesh,
        in_specs=(
            P("delay", "rows", None, None, None),
            P("delay", "rows", None, None),
            P("delay", "rows", None),
            P("rows", None, None),
            P(None, "rows", None, None),
            P("delay", "rows", None, None),
        ),
        out_specs=P(None, "rows", None, None),
        check_vma=False,
    )
```

```python
import functools

import jax
import jax.numpy as jnp
from jax import lax
from jax.experimental import pallas as pl
from jax.experimental.pallas import tpu as pltpu
from jax.sharding import PartitionSpec as P


STEPS = 4
LANES = 16
ROWS = 16
CAP = 8
NB = 64
EXC = 4
B = 128
L = 4
TAKEN = ROWS * CAP
FLAT = NB * EXC
KNOWN = 3
GIVERS = (4, 9)
SHARE = FLAT // LANES
GROUP = 16

bf16 = jnp.bfloat16
f32 = jnp.float32
VMEM = pl.BlockSpec(memory_space=pltpu.VMEM)
SMEM = pl.BlockSpec(memory_space=pltpu.SMEM)
HBM = pl.BlockSpec(memory_space=pltpu.HBM)
LIMIT = 16 * 1024 * 1024


def call(kernel, out_shape, scratch, operands, in_smem, in_place=(), out_in_place=False):
    specs = [SMEM if i in in_smem else HBM if i in in_place else VMEM for i in range(len(operands))]
    many = isinstance(out_shape, (tuple, list))
    operands = [pltpu.with_memory_space_constraint(x, pltpu.HBM) if i in in_place else x for i, x in enumerate(operands)]
    return pl.pallas_call(
        kernel,
        out_shape=out_shape,
        in_specs=specs,
        out_specs=[VMEM] * len(out_shape) if many else (HBM if out_in_place else VMEM),
        scratch_shapes=scratch,
        compiler_params=pltpu.CompilerParams(vmem_limit_bytes=LIMIT),
    )(*operands)


def pick_initial(listed, stored, tiles, h1, h2, out, h0, asked, sem, list_sem):
    copy = pltpu.make_async_copy(stored, h0, sem)
    copy.start()
    fetch = pltpu.make_async_copy(listed, asked, list_sem)
    fetch.start()
    fetch.wait()
    for r in range(ROWS):
        for p in range(CAP):
            at = asked[r, p]
            out[r, CAP + p] = h1[at]
            out[r, 2 * CAP + p] = h2[at]
    copy.wait()
    for r in range(ROWS):
        for p in range(CAP):
            out[r, p] = h0[asked[r, p]]


def initial_terms(listed, tiles, arrived, out, wide, packed, total, slots, sem):
    fetch = pltpu.make_async_copy(listed, slots, sem)
    fetch.start()
    for o in range(ROWS):
        for t in range(KNOWN):
            here = arrived[o, CAP * t : CAP * (t + 1)]
            wide[CAP * o : CAP * (o + 1), EXC * t : EXC * (t + 1), :] = here.astype(f32)
    packed[...] = wide[...].astype(bf16)
    fetch.wait()
    for i in range(NB):
        row = jnp.concatenate([packed[slots[s, i]] for s in range(L)], axis=1)
        tile = tiles[i].reshape(L * B, B)
        term = jnp.dot(row, tile, preferred_element_type=f32)
        for t in range(KNOWN):
            total[t, EXC * i : EXC * (i + 1), :] = term[EXC * t : EXC * (t + 1)]

    for y in range(4):
        out[y] = total[y % KNOWN].astype(bf16)


def add_terms(terms, out):
    total = sum(terms[y].astype(f32) for y in range(4)).astype(bf16)
    for x in range(4):
        out[x] = total


def solve(driven, diag, solved):
    for i in range(NB):
        row = driven[EXC * i : EXC * (i + 1), :].astype(bf16)
        solved[i] = jnp.dot(row, diag[i], preferred_element_type=f32)


def pick(fetch, asked, solved, send):
    fetch.wait()
    for r in range(ROWS):
        for p in range(CAP):
            send[r, p] = solved[asked[r, p]].astype(bf16)


def older(h2, item):
    for i in range(NB):
        item[EXC * i : EXC * (i + 1), :] = h2[i].astype(f32)


def first_step(listed, terms, h2, excite, diag, moved, item, send, driven, solved, asked, sem):
    fetch = pltpu.make_async_copy(listed, asked, sem)
    me = lax.axis_index("delay")

    @pl.when(me < 2)
    def _():
        fetch.start()

    whole = sum(terms[x].astype(f32) for x in range(4))
    driven[...] = excite[0] - whole
    gives = (me == GIVERS[0]) | (me == GIVERS[1])

    @pl.when(gives)
    def _():
        moved[...] = whole

    @pl.when(jnp.logical_not(gives) & (me > 1))
    def _():
        older(h2, moved)

    item[...] = driven[...].astype(bf16)

    @pl.when(me < 2)
    def _():
        solve(driven, diag, solved)
        pick(fetch, asked, solved, send)


def tile_terms(slots, tiles, arrived, total):
    for i in range(NB):
        row = jnp.concatenate([arrived[slots[s, i]] for s in range(L)], axis=1)
        tile = tiles[i].reshape(L * B, B)
        total[EXC * i : EXC * (i + 1), :] = jnp.dot(row, tile, preferred_element_type=f32)


def tile_terms_below(lanes, slots, tiles, arrived, total):
    @pl.when(lax.axis_index("delay") < lanes)
    def _():
        tile_terms(slots, tiles, arrived, total)


def second_step(listed, total, came, h2, excite, diag, item, send, driven, solved, asked, sem):
    fetch = pltpu.make_async_copy(listed, asked, sem)
    me = lax.axis_index("delay")

    @pl.when(me == 0)
    def _():
        fetch.start()

    value = total[...] + came[...]
    driven[...] = excite[1] - value

    @pl.when(me == 0)
    def _():
        item[...] = driven[...].astype(bf16).astype(f32)
        solve(driven, diag, solved)
        pick(fetch, asked, solved, send)

    @pl.when(me == 1)
    def _():
        item[...] = value

    @pl.when(me > 1)
    def _():
        older(h2, item)


def third_step(listed, total, came, before, first, excite, diag, item, send, driven, solved, asked, sem):
    fetch = pltpu.make_async_copy(listed, asked, sem)
    fetch.start()
    me = lax.axis_index("delay")
    late = (me == 1) | (me == GIVERS[0] + 1) | (me == GIVERS[1] + 1)
    other = jnp.where(me == 2, first[...].astype(f32), jnp.where(late, came[...], before[...]))
    driven[...] = jnp.where(me == 0, excite[2] - (total[...] + came[...]), other)
    item[...] = driven[...].astype(bf16)

    @pl.when(me < KNOWN)
    def _():
        solve(driven, diag, solved)

    @pl.when(me >= KNOWN)
    def _():
        for i in range(NB):
            solved[i] = driven[EXC * i : EXC * (i + 1), :]

    pick(fetch, asked, solved, send)


def fourth_step(slots, tiles, arrived, item, out, total):
    tile_terms(slots, tiles, arrived, total)
    for k in range(LANES):
        mine = slice(SHARE * k, SHARE * (k + 1))
        out[k, :SHARE] = total[mine, :].astype(bf16)
        out[k, SHARE:] = item[mine, :]


def share_driven(parts, excite, out, rows):
    total = parts[0, :SHARE].astype(f32)
    for k in range(1, LANES):
        total = total + parts[k, :SHARE].astype(f32)
    start = pl.multiple_of(lax.axis_index("delay") * SHARE, SHARE)
    last = excite[STEPS - 1, pl.ds(start, SHARE), :] - total
    values = [parts[STEPS - 2 - t, SHARE:].astype(f32) for t in range(STEPS - 1)] + [last]
    for t, value in enumerate(values):
        for b in range(SHARE // EXC):
            at = EXC * (STEPS * b + t)
            rows[at : at + EXC] = value[EXC * b : EXC * (b + 1)]
    both = rows[...].astype(bf16)
    for k in range(LANES):
        out[k] = both


def last_solve(driven, diag, stored, out, sems):
    each = SHARE // EXC
    copies = []
    for i in range(NB):
        mine = slice(EXC * STEPS * (i % each), EXC * STEPS * (i % each + 1))
        value = jnp.dot(driven[i // each, mine], diag[i], preferred_element_type=f32)
        for t in range(STEPS):
            out[t, i] = value[EXC * t : EXC * (t + 1)]
        if i % GROUP == GROUP - 1:
            part = (slice(None), pl.ds(i - GROUP + 1, GROUP))
            copies.append(pltpu.make_async_copy(out.at[part], stored.at[part], sems.at[len(copies)]))
            copies[-1].start()
    for copy in copies:
        copy.wait()


def shifted(array, axis, by):
    peers = lax.axis_size(axis)
    return lax.ppermute(array, axis, [(i, i + by) for i in range(peers - by)])


def exchange(array, axis, groups=None):
    return lax.all_to_all(array, axis, split_axis=0, concat_axis=0, tiled=True, axis_index_groups=groups)


def body(retarded_tiles, wanted_blocks, tile_slots, diag_inverse, excitation, history_init):
    sds = jax.ShapeDtypeStruct
    tiles = retarded_tiles[0]
    slots = tile_slots[0].T
    excite = excitation.reshape(STEPS, FLAT, B)

    asked = exchange(wanted_blocks[0, 0], "rows")
    h0 = history_init[0]
    later = []
    for t in range(1, KNOWN):
        later.append(shifted(h0, "delay", t))

    picked = call(
        pick_initial,
        sds((ROWS, KNOWN * CAP, EXC, B), bf16),
        [
            pltpu.VMEM(h0.shape, bf16),
            pltpu.SMEM((ROWS, CAP), jnp.int32),
            pltpu.SemaphoreType.DMA,
            pltpu.SemaphoreType.DMA,
        ],
        (asked, h0, tiles, *later),
        (),
        (1, 2),
    )
    arrived = exchange(picked, "rows")
    wide = (TAKEN, EXC * STEPS, B)
    terms = call(
        initial_terms,
        sds((4, FLAT, B), bf16),
        [
            pltpu.VMEM(wide, f32),
            pltpu.VMEM(wide, bf16),
            pltpu.VMEM((KNOWN, FLAT, B), f32),
            pltpu.SMEM(slots.shape, jnp.int32),
            pltpu.SemaphoreType.DMA,
        ],
        (slots, tiles, arrived),
        (),
    )
    along_x = [[4 * y + x for x in range(4)] for y in range(4)]
    along_y = [[4 * y + x for y in range(4)] for x in range(4)]
    terms = exchange(terms, "delay", along_y)
    terms = call(add_terms, sds((4, FLAT, B), bf16), [], (terms,), ())
    terms = exchange(terms, "delay", along_x)

    flat = pltpu.VMEM((FLAT, B), f32)
    block = pltpu.VMEM((NB, EXC, B), f32)
    work = [flat, block, pltpu.SMEM((ROWS, CAP), jnp.int32), pltpu.SemaphoreType.DMA]
    send_shape = sds((ROWS, CAP, EXC, B), bf16)

    moved, item0, send = call(
        first_step,
        (sds((FLAT, B), f32), sds((FLAT, B), bf16), send_shape),
        work,
        (asked, terms, later[1], excite, diag_inverse),
        (),
    )
    steps = [(k, k + 1) for k in range(2, LANES - 1)]
    pairs = [(k, j) for k, j in steps if k not in GIVERS]
    before = lax.ppermute(moved, "delay", [(GIVERS[0], 0), (GIVERS[1], 1)] + pairs)
    arrived = exchange(send, "rows").reshape(TAKEN, EXC, B)
    total = call(functools.partial(tile_terms_below, 2), sds((FLAT, B), f32), [], (slots, tiles, arrived), (0,))

    item1, send = call(
        second_step, (sds((FLAT, B), f32), send_shape), work, (asked, total, before, later[1], excite, diag_inverse), ()
    )
    came = lax.ppermute(item1, "delay", [(0, 1), (1, 0)] + [(k, j) for k, j in steps if k in GIVERS])
    arrived = exchange(send, "rows").reshape(TAKEN, EXC, B)
    total = call(functools.partial(tile_terms_below, 1), sds((FLAT, B), f32), [], (slots, tiles, arrived), (0,))

    item2, send = call(
        third_step,
        (sds((FLAT, B), bf16), send_shape),
        work,
        (asked, total, came, before, item0, excite, diag_inverse),
        (),
    )
    arrived = exchange(send, "rows").reshape(TAKEN, EXC, B)
    parts = call(fourth_step, sds((LANES, 2 * SHARE, B), bf16), [flat], (slots, tiles, arrived, item2), (0,))
    parts = exchange(parts, "delay")
    shares = call(
        share_driven, sds((LANES, STEPS * SHARE, B), bf16), [pltpu.VMEM((STEPS * SHARE, B), f32)], (parts, excite), ()
    )
    driven = exchange(shares, "delay")
    final = (STEPS, NB, EXC, B)
    return call(
        last_solve,
        sds(final, f32),
        [pltpu.VMEM(final, f32), pltpu.SemaphoreType.DMA((NB // GROUP,))],
        (driven, diag_inverse),
        (),
        out_in_place=True,
    )


def solution(mesh):
    return jax.shard_map(
        body,
        mesh=mesh,
        in_specs=(
            P("delay", "rows", None, None, None),
            P("delay", "rows", None, None),
            P("delay", "rows", None),
            P("rows", None, None),
            P(None, "rows", None, None),
            P("delay", "rows", None, None),
        ),
        out_specs=P(None, "rows", None, None),
        check_vma=False,
    )
```
